32 devices in a mesh: dp: 8 (over y, x, core), tensor: 4 (over z).
Axes of the slice: x: 2, y: 2, z: 4, core: 2. Of those that a mesh axis runs over, the one named last changes fastest.
Arguments:
- hidden_states: float32 [2048, 1024], P('dp'), may hold values from -6 to 6
- output_cotangent: float32 [2048, 1024], P('dp'), may hold values from -6 to 6
- routes: int32 [2048, 8], P('dp'), may hold values from 0 to 31, all different within a row; in each aligned block of 256 rows (0 to 255, 256 to 511, ...) at most 96 rows name the same one
- attention_gain: float32 [2, 1024], replicated, may hold values from 0.5 to 1.5
- query_weight: bfloat16 [2, 1024, 1024], P(None, None, 'tensor'), may hold values from -0.1875 to 0.1875
- key_weight: bfloat16 [2, 512, 1024], P(None, 'tensor'), may hold values from -0.1875 to 0.1875
- value_weight: bfloat16 [2, 512, 1024], P(None, 'tensor'), may hold values from -0.1875 to 0.1875
- output_weight: bfloat16 [2, 1024, 1024], P(None, 'tensor'), may hold values from -4 to 4
- mixture_gain: float32 [2, 1024], replicated, may hold values from 0.5 to 1.5
- router_weight: bfloat16 [2, 1024, 32], replicated, may hold values from -0.046875 to 0.046875
- gate_weight: bfloat16 [2, 32, 512, 1024], P(None, 'dp', 'tensor'), may hold values from -0.1875 to 0.1875
- up_weight: bfloat16 [2, 32, 512, 1024], P(None, 'dp', 'tensor'), may hold values from -0.1875 to 0.1875
- down_weight: bfloat16 [2, 32, 512, 1024], P(None, 'dp', 'tensor'), may hold values from -6 to 6
Outputs:
- block_output: float32 [2048, 1024], P('dp')
- input_gradient: float32 [2048, 1024], P('dp')
- attention_gain_gradient: float32 [2, 1024], P(None, 'dp')
- query_gradient: float32 [2, 1024, 1024], P(None, 'dp', 'tensor')
- key_gradient: float32 [2, 512, 1024], P(None, 'tensor', 'dp')
- value_gradient: float32 [2, 512, 1024], P(None, 'tensor', 'dp')
- projection_gradient: float32 [2, 1024, 1024], P(None, 'tensor', 'dp')
- mixture_gain_gradient: float32 [2, 1024], P(None, 'dp')
- router_gradient: float32 [2, 1024, 32], P(None, 'dp')
- gate_gradient: float32 [2, 32, 512, 1024], P(None, 'dp', 'tensor')
- up_gradient: float32 [2, 32, 512, 1024], P(None, 'dp', 'tensor')
- down_gradient: float32 [2, 32, 512, 1024], P(None, 'dp', 'tensor')
The draws below stay inside these ranges and needn't reach their ends.
Inputs may be any that keep to these rules, and one draw needn't show every extreme that they name: `routes`: each row names 8 different experts; among the rows of one block of 256 rows no expert is named more than 96 times, a bound that some block reaches.
All inputs are finite; a program needn't handle non-finite values.
Results may differ from the reference program's by a relative error of at most 0.02.
Values may be sent and summed in bfloat16 or wider, within the bound.
A program may use at most 256 MiB of HBM per device.

```python
import math
import jax
import jax.numpy as jnp
import numpy as np
from jax import lax

D = 1024
H = 16
KV = 8
HD = 64
EXPERTS = 32
FF = 512
TOPK = 8
LAYERS = 2
SEQ = 256
TOK_DEV = 256
TOKENS = 2048
CAP = 96
N_DP = 8


def with_spikes(entries, own_key, source, target, parts, factor):
    owner, partner = [(jnp.arange(entries.shape[dim]) // (entries.shape[dim] // parts)).reshape([-1 if axis == dim else 1 for axis in range(entries.ndim)]) for dim in (source, target)]
    chosen = jax.random.permutation(own_key, parts)[partner]
    strong = (owner == chosen) | (owner == (partner + parts // 2) % parts)
    return jnp.where(strong, factor * entries, entries)


def steps_of(key, shape, shards, low, top_value):
    factor_of = 1.0
    for dim, blocks in shards:
        draws = jax.random.uniform(jax.random.fold_in(jax.random.fold_in(key, 6), dim), (blocks,), jnp.float32, low / len(shards), top_value / len(shards))
        factor_of = factor_of * jnp.repeat(jnp.exp(draws), shape[dim] // blocks).reshape((-1,) + (1,) * (len(shape) - 1 - dim))
    return factor_of


def routed_block(stream_key, own, number, rows, number_of, top, limit, lean):
    order = jax.random.permutation(stream_key, number_of)
    crowded, common = portions_of(number_of, rows * top, limit, lean, True), portions_of(number_of, rows * top, limit, lean, False)
    places = jnp.arange(number_of)

    def named(sizes, turn):
        used = int((sizes > 0).sum())
        fixed = max(1, used // 4)
        moved = fixed + (places - fixed + turn * (used - fixed)) % max(1, number_of - fixed)
        return jnp.zeros((number_of,), jnp.int32).at[order[jnp.where(places < fixed, places, moved)]].set(jnp.asarray(sizes, jnp.int32))

    sizes = jnp.where(number % 4 == 0, named(crowded, number // 4), named(common, number - number // 4 - 1))
    mixed = jax.random.permutation(jax.random.fold_in(own, 3), number_of)
    giver, taker = mixed[0:number_of // 2 * 2:2], mixed[1:number_of // 2 * 2:2]
    margin = jnp.minimum(sizes[giver] - 1, limit - sizes[taker]) // 2
    margin = jnp.where((giver == order[0]) | (taker == order[0]) | (sizes[taker] == 0), 0, jnp.maximum(margin, 0))
    moved = jax.random.randint(jax.random.fold_in(own, 4), (number_of // 2,), 0, 1 << 20) % (margin + 1)
    sizes = sizes.at[giver].add(-moved).at[taker].add(moved)
    items = jnp.searchsorted(jnp.cumsum(sizes), jnp.arange(rows * top), side="right").astype(jnp.int32)
    listing = items.reshape(top, rows).T
    listing = listing[jax.random.permutation(jax.random.fold_in(own, 1), rows)]
    turn = jax.random.randint(jax.random.fold_in(own, 2), (rows, 1), 0, top)
    return jnp.take_along_axis(listing, (jnp.arange(top)[None, :] + turn) % top, axis=1)


def portions_of(number_of, total, reach, skew, full):
    weights = [(1 << 20) // math.isqrt(rank ** skew) + 1 for rank in range(1, number_of + 1)]
    largest = reach if full else min(reach, max(-(-total // number_of), total * weights[0] // sum(weights)))
    least = 1 if total - largest >= number_of - 1 else 0
    given, spare = [largest] + [least] * (number_of - 1), total - largest - least * (number_of - 1)
    while spare > 0:
        candidates = [i for i in range(1, number_of) if given[i] < largest] or [i for i in range(1, number_of) if given[i] < reach]
        whole, remaining = sum([weights[i] for i in candidates]), spare
        for i in candidates:
            addition = min(reach - given[i], max(1, remaining * weights[i] // whole), spare)
            given[i] = given[i] + addition
            spare = spare - addition
    return np.array(given)


def noise(key, dims, scale, most, cuts=(), kind=jnp.bfloat16):
    factor_of = steps_of(key, dims, cuts, -0.22, 0.18) if cuts else 1.0
    array = jax.random.normal(key, dims, jnp.float32) * scale * factor_of
    return jnp.minimum(jnp.maximum(array, -most), most).astype(kind)


def noise_with(own_key, shape, deviation, reach, cuts, heavy, held_as=jnp.bfloat16):
    values = deviation * jax.random.normal(own_key, shape, jnp.float32)
    if cuts:
        values = values * steps_of(own_key, shape, cuts, -0.22, 0.18)
    return jnp.clip(with_spikes(values, jax.random.fold_in(own_key, 3), *heavy), -reach, reach).astype(held_as)


def setup_inputs(seed: int = 0) -> dict:
    key_list = jax.random.split(jax.random.key(seed), 14)
    hidden_states = noise_with(key_list[0], (TOKENS, D), 1.0, 6.0, ((0, 8),), (0, 1, 8, 2.0), jnp.float32)
    output_cotangent = noise_with(key_list[1], (TOKENS, D), 1.0, 6.0, ((0, 8),), (0, 1, 8, 2.0), jnp.float32)
    routes_keys = jax.random.split(jax.random.fold_in(key_list[2], 1), TOKENS // TOK_DEV)
    routes_turns = jax.random.permutation(jax.random.fold_in(key_list[2], 3), TOKENS // TOK_DEV)
    routes = jax.vmap(lambda own, number: routed_block(jax.random.fold_in(key_list[2], 2), own, number, TOK_DEV, EXPERTS, TOPK, CAP, 2))(routes_keys, routes_turns).reshape((TOKENS, TOPK))
    attention_gain = jnp.clip(1.0 + 0.1 * jax.random.normal(key_list[3], (LAYERS, D), jnp.float32), 0.5, 1.5)
    query_weight = noise(key_list[4], (LAYERS, D, H * HD), D ** -0.5, 0.1875, ((2, 4),))
    key_weight = noise(key_list[5], (LAYERS, KV * HD, D), D ** -0.5, 0.1875, ((1, 4),))
    value_weight = noise(key_list[6], (LAYERS, KV * HD, D), D ** -0.5, 0.1875, ((1, 4),))
    output_weight = noise(key_list[7], (LAYERS, H * HD, D), 2 ** -0.5, 4.0, ((1, 4),))
    mixture_gain = jnp.clip(1.0 + 0.1 * jax.random.normal(key_list[8], (LAYERS, D), jnp.float32), 0.5, 1.5)
    router_weight = noise(key_list[9], (LAYERS, D, EXPERTS), (16 * D) ** -0.5, 0.046875)
    gate_weight = noise(key_list[10], (LAYERS, EXPERTS, FF, D), D ** -0.5, 0.1875, ((1, 8), (2, 4)))
    up_weight = noise(key_list[11], (LAYERS, EXPERTS, FF, D), D ** -0.5, 0.1875, ((1, 8), (2, 4)))
    down_weight = noise(key_list[12], (LAYERS, EXPERTS, FF, D), 1 ** -0.5, 6.0, ((1, 8), (2, 4)))
    return {"hidden_states": hidden_states, "output_cotangent": output_cotangent, "routes": routes, "attention_gain": attention_gain, "query_weight": query_weight, "key_weight": key_weight, "value_weight": value_weight, "output_weight": output_weight, "mixture_gain": mixture_gain, "router_weight": router_weight, "gate_weight": gate_weight, "up_weight": up_weight, "down_weight": down_weight}


EPSILON = 1e-06
RESIDUAL_SCALE = 0.22
SCORE_SCALE = 0.015625
ROPE_BASE = 10000.0
NEG_LARGE = -1e+30

def rotate_half(values):
    middle = values.shape[-1] // 2
    return jnp.concatenate([-values[..., middle:], values[..., :middle]], axis=-1)

def rope_tables(row_count):
    middle = HD // 2
    positions = (jnp.arange(row_count, dtype=jnp.int32) % SEQ).astype(jnp.float32)
    inverse_rate = ROPE_BASE ** (-(jnp.arange(middle, dtype=jnp.int32).astype(jnp.float32) * (2.0 / HD)))
    angles = positions[:, None] * inverse_rate[None, :]
    cosine = jnp.concatenate([jnp.cos(angles), jnp.cos(angles)], axis=1)[:, None, :]
    sine = jnp.concatenate([jnp.sin(angles), jnp.sin(angles)], axis=1)[:, None, :]
    return (cosine, sine)

def causal_mask():
    counter = jnp.arange(SEQ, dtype=jnp.int32)
    return counter[:, None] >= counter[None, :]

def dot_full(left, right):
    return jnp.dot(left, right, precision=lax.Precision.HIGHEST, preferred_element_type=jnp.float32)

def float_einsum(form, left, right):
    return jnp.einsum(form, left.astype(jnp.float32), right.astype(jnp.float32), preferred_element_type=jnp.float32)

def slot_targets(routes, experts):
    flat_routes = routes.reshape(-1)
    onehot = (flat_routes[:, None] == jnp.arange(experts, dtype=jnp.int32)[None, :]).astype(jnp.int32)
    before = jnp.cumsum(onehot, axis=0) - onehot
    slot_index = lax.optimization_barrier(jnp.sum(before * onehot, axis=1))
    return (flat_routes * CAP + slot_index).astype(jnp.int32).reshape(routes.shape)

def norm_forward(source, gain):
    inverse_root = lax.rsqrt(lax.optimization_barrier(jnp.mean(source * source, axis=1, keepdims=True)) + EPSILON)
    return (inverse_root, source * inverse_root * gain)

def norm_backward(grad_in, source, inverse_root, gain):
    gain_grad = lax.optimization_barrier(jnp.sum(grad_in * source * inverse_root, axis=0))
    scaled = grad_in * gain
    inner = lax.optimization_barrier(jnp.mean(scaled * source, axis=1, keepdims=True))
    return (inverse_root * (scaled - source * inverse_root * inverse_root * inner), gain_grad)

def attend_forward(query, keys, values):
    scores = float_einsum('sqkgd,stkd->skgqt', query, keys) * SCORE_SCALE
    scores = jnp.where(causal_mask(), scores, NEG_LARGE)
    highest = lax.optimization_barrier(jnp.max(scores, axis=-1, keepdims=True))
    weights = jnp.exp(scores - highest)
    totals = lax.optimization_barrier(jnp.sum(weights, axis=-1, keepdims=True))
    log_total = highest + jnp.log(totals)
    probability = (weights / totals).astype(jnp.bfloat16)
    attended = float_einsum('skgqt,stkd->sqkgd', probability, values)
    return (attended.astype(jnp.bfloat16), log_total)

def attend_backward(query, keys, values, attended, log_total, grad_out):
    scores = float_einsum('sqkgd,stkd->skgqt', query, keys) * SCORE_SCALE
    scores = jnp.where(causal_mask(), scores, NEG_LARGE)
    probability = jnp.exp(scores - log_total)
    value_grad = float_einsum('skgqt,sqkgd->stkd', probability.astype(jnp.bfloat16), grad_out)
    prob_grad = float_einsum('sqkgd,stkd->skgqt', grad_out, values)
    delta_rows = lax.optimization_barrier(jnp.sum(grad_out.astype(jnp.float32) * attended.astype(jnp.float32), axis=-1))
    delta_rows = jnp.transpose(delta_rows, (0, 2, 3, 1))[..., None]
    score_grad = (probability * (prob_grad - delta_rows)).astype(jnp.bfloat16)
    query_grad = float_einsum('skgqt,stkd->sqkgd', score_grad, keys) * SCORE_SCALE
    key_grad = float_einsum('skgqt,sqkgd->stkd', score_grad, query) * SCORE_SCALE
    return (query_grad, key_grad, value_grad)

def router_backward(weight_grad, router_probs, chosen):
    prob_grad = lax.optimization_barrier(jnp.sum(chosen * weight_grad[:, :, None], axis=1))
    return router_probs * (prob_grad - lax.optimization_barrier(jnp.sum(router_probs * prob_grad, axis=1, keepdims=True)))

def layer_forward(inputs, params, targets, chosen, cosine, sine):
    attention_gain, query_weight, key_weight, value_weight, output_weight, mixture_gain, router_weight, gate_weight, up_weight, down_weight = params
    row_count, width = inputs.shape
    query_heads = query_weight.shape[1] // HD
    key_heads = key_weight.shape[0] // HD
    group_size = query_heads // key_heads
    seq_count = row_count // SEQ
    first_scale, first_normed = norm_forward(inputs, attention_gain)
    first_input = first_normed.astype(jnp.bfloat16)
    query = jnp.dot(first_input, query_weight, preferred_element_type=jnp.float32).reshape(row_count, query_heads, HD)
    keys = jnp.dot(first_input, key_weight.T, preferred_element_type=jnp.float32).reshape(row_count, key_heads, HD)
    values = jnp.dot(first_input, value_weight.T, preferred_element_type=jnp.float32).astype(jnp.bfloat16)
    query = (query * cosine + rotate_half(query) * sine).astype(jnp.bfloat16)
    keys = (keys * cosine + rotate_half(keys) * sine).astype(jnp.bfloat16)
    query_split = query.reshape(seq_count, SEQ, key_heads, group_size, HD)
    key_split = keys.reshape(seq_count, SEQ, key_heads, HD)
    value_split = values.reshape(seq_count, SEQ, key_heads, HD)
    attended, log_total = attend_forward(query_split, key_split, value_split)
    attended_rows = attended.reshape(row_count, query_heads * HD)
    attention_out = jnp.dot(attended_rows, output_weight, preferred_element_type=jnp.float32)
    middle_state = inputs + RESIDUAL_SCALE * attention_out
    second_scale, second_normed = norm_forward(middle_state, mixture_gain)
    second_input = second_normed.astype(jnp.bfloat16)
    logits = jnp.dot(second_input, router_weight, preferred_element_type=jnp.float32)
    router_probs = jax.nn.softmax(logits, axis=1)
    route_weights = lax.optimization_barrier(jnp.sum(chosen * router_probs[:, None, :], axis=2))
    experts = gate_weight.shape[0]
    flat_targets = targets.reshape(-1)
    dispatched = jnp.zeros((experts * CAP, width), jnp.bfloat16).at[flat_targets].set(jnp.repeat(second_input, TOPK, axis=0)).reshape(experts, CAP, width)
    gate_pre = float_einsum('ecd,efd->ecf', dispatched, gate_weight)
    up_pre = float_einsum('ecd,efd->ecf', dispatched, up_weight)
    activated = (jax.nn.silu(gate_pre) * up_pre).astype(jnp.bfloat16)
    expert_out = float_einsum('ecf,efd->ecd', activated, down_weight).reshape(experts * CAP, width)
    picked = expert_out[targets]
    mixture_out = lax.optimization_barrier(jnp.sum(route_weights[:, :, None] * picked, axis=1))
    outputs = middle_state + RESIDUAL_SCALE * mixture_out
    saved = (first_scale, first_input, query_split, key_split, value_split, attended, log_total, middle_state, second_scale, second_input, router_probs, route_weights, dispatched, gate_pre, up_pre, activated, picked)
    return (outputs, saved)

def layer_backward(grad_out, saved, params, targets, chosen, cosine, sine, inputs):
    attention_gain, query_weight, key_weight, value_weight, output_weight, mixture_gain, router_weight, gate_weight, up_weight, down_weight = params
    first_scale, first_input, query_split, key_split, value_split, attended, log_total, middle_state, second_scale, second_input, router_probs, route_weights, dispatched, gate_pre, up_pre, activated, picked = saved
    row_count, width = grad_out.shape
    query_heads = query_weight.shape[1] // HD
    key_heads = key_weight.shape[0] // HD
    experts = gate_weight.shape[0]
    mixture_grad = RESIDUAL_SCALE * grad_out
    weight_grad = lax.optimization_barrier(jnp.sum(mixture_grad[:, None, :] * picked, axis=2))
    spread = (route_weights[:, :, None] * mixture_grad[:, None, :]).astype(jnp.bfloat16).reshape(row_count * TOPK, width)
    out_grad = jnp.zeros((experts * CAP, width), jnp.bfloat16).at[targets.reshape(-1)].set(spread).reshape(experts, CAP, width)
    act_grad = float_einsum('ecd,efd->ecf', out_grad, down_weight)
    down_grad = float_einsum('ecf,ecd->efd', activated, out_grad)
    sigma = jax.nn.sigmoid(gate_pre)
    gate_rows = (act_grad * up_pre * sigma * (1.0 + gate_pre * (1.0 - sigma))).astype(jnp.bfloat16)
    up_rows = (act_grad * gate_pre * sigma).astype(jnp.bfloat16)
    gate_grad = float_einsum('ecf,ecd->efd', gate_rows, dispatched)
    up_grad = float_einsum('ecf,ecd->efd', up_rows, dispatched)
    dispatch_grad = (float_einsum('ecf,efd->ecd', gate_rows, gate_weight) + float_einsum('ecf,efd->ecd', up_rows, up_weight)).reshape(experts * CAP, width)
    input_part = lax.optimization_barrier(jnp.sum(dispatch_grad[targets], axis=1))
    logit_grad = router_backward(weight_grad, router_probs, chosen)
    second_grad = input_part + dot_full(logit_grad, router_weight.astype(jnp.float32).T)
    router_grad = dot_full(second_input.astype(jnp.float32).T, logit_grad)
    middle_norm_grad, mixture_gain_grad = norm_backward(second_grad, middle_state, second_scale, mixture_gain)
    middle_grad = grad_out + middle_norm_grad
    attention_grad = (RESIDUAL_SCALE * middle_grad).astype(jnp.bfloat16)
    attended_rows = attended.reshape(row_count, query_heads * HD)
    output_grad = jnp.dot(attended_rows.T, attention_grad, preferred_element_type=jnp.float32)
    attended_grad = jnp.dot(attention_grad, output_weight.T, preferred_element_type=jnp.float32).astype(jnp.bfloat16)
    query_grad, key_grad, value_grad = attend_backward(query_split, key_split, value_split, attended, log_total, attended_grad.reshape(attended.shape))
    query_grad = query_grad.reshape(row_count, query_heads, HD)
    query_grad = (query_grad * cosine - rotate_half(query_grad) * sine).astype(jnp.bfloat16).reshape(row_count, query_heads * HD)
    key_grad = key_grad.reshape(row_count, key_heads, HD)
    key_grad = (key_grad * cosine - rotate_half(key_grad) * sine).astype(jnp.bfloat16).reshape(row_count, key_heads * HD)
    value_grad = value_grad.astype(jnp.bfloat16).reshape(row_count, key_heads * HD)
    query_weight_grad = jnp.dot(first_input.T, query_grad, preferred_element_type=jnp.float32)
    key_weight_grad = jnp.dot(key_grad.T, first_input, preferred_element_type=jnp.float32)
    value_weight_grad = jnp.dot(value_grad.T, first_input, preferred_element_type=jnp.float32)
    first_grad = jnp.dot(query_grad, query_weight.T, preferred_element_type=jnp.float32) + jnp.dot(key_grad, key_weight, preferred_element_type=jnp.float32) + jnp.dot(value_grad, value_weight, preferred_element_type=jnp.float32)
    input_norm_grad, attention_gain_grad = norm_backward(first_grad, inputs, first_scale, attention_gain)
    input_grad = middle_grad + input_norm_grad
    return (input_grad, (attention_gain_grad, query_weight_grad, key_weight_grad, value_weight_grad, output_grad, mixture_gain_grad, router_grad, gate_grad, up_grad, down_grad))

def reference(hidden_states, output_cotangent, routes, attention_gain, query_weight, key_weight, value_weight, output_weight, mixture_gain, router_weight, gate_weight, up_weight, down_weight):
    params_all = (attention_gain, query_weight, key_weight, value_weight, output_weight, mixture_gain, router_weight, gate_weight, up_weight, down_weight)
    cosine, sine = rope_tables(TOK_DEV)

    def one_block(totals, block):
        states, cotangent, block_routes = block
        targets = slot_targets(block_routes, EXPERTS)
        chosen = (block_routes[:, :, None] == jnp.arange(EXPERTS, dtype=jnp.int32)[None, None, :]).astype(jnp.float32)
        current = states
        kept = []
        for layer_index in range(LAYERS):
            layer_params = tuple((weight[layer_index] for weight in params_all))
            layer_input = current
            current, saved = layer_forward(current, layer_params, targets, chosen, cosine, sine)
            kept.append((saved, layer_input))
        grad_now = cotangent
        per_layer = [None] * LAYERS
        for layer_index in reversed(range(LAYERS)):
            layer_params = tuple((weight[layer_index] for weight in params_all))
            grad_now, grads = layer_backward(grad_now, kept[layer_index][0], layer_params, targets, chosen, cosine, sine, kept[layer_index][1])
            per_layer[layer_index] = grads
        new_totals = tuple((totals[position] + jnp.stack([entry[position] for entry in per_layer]) for position in range(10)))
        return (new_totals, (current, grad_now))
    zero_totals = tuple((jnp.zeros(weight.shape, jnp.float32) for weight in params_all))
    blocks = (hidden_states.reshape(N_DP, TOK_DEV, D), output_cotangent.reshape(N_DP, TOK_DEV, D), routes.reshape(N_DP, TOK_DEV, TOPK))
    totals, (outputs, gradients) = lax.scan(one_block, zero_totals, blocks)
    return (outputs.reshape(TOKENS, D), gradients.reshape(TOKENS, D), totals[0], totals[1], totals[2], totals[3], totals[4], totals[5], totals[6], totals[7], totals[8], totals[9])
```

```python
import functools

import jax
import jax.numpy as jnp
from jax import lax
from jax.experimental import pallas as pl
from jax.experimental.pallas import tpu as pltpu
from jax.sharding import PartitionSpec as P

HD = 64
EXPERTS = 32
SEQ = 256


EPSILON = 1e-06
RESIDUAL_SCALE = 0.22
SCORE_SCALE = 0.015625
ROPE_BASE = 10000.0
NEG_LARGE = -1e30


def rotate_half(values):
    middle = values.shape[-1] // 2
    return jnp.concatenate([-values[..., middle:], values[..., :middle]], axis=-1)


def rope_tables(row_count):
    middle = HD // 2
    positions = (jnp.arange(row_count, dtype=jnp.int32) % SEQ).astype(jnp.float32)
    inverse_rate = ROPE_BASE ** (
        -(jnp.arange(middle, dtype=jnp.int32).astype(jnp.float32) * (2.0 / HD))
    )
    angles = positions[:, None] * inverse_rate[None, :]
    cosine = jnp.concatenate([jnp.cos(angles), jnp.cos(angles)], axis=1)[:, None, :]
    sine = jnp.concatenate([jnp.sin(angles), jnp.sin(angles)], axis=1)[:, None, :]
    return (cosine, sine)


def causal_mask():
    counter = jnp.arange(SEQ, dtype=jnp.int32)
    return counter[:, None] >= counter[None, :]


def dot_full(left, right):
    return jnp.dot(left, right, precision=lax.Precision.HIGHEST, preferred_element_type=jnp.float32)


def norm_forward(source, gain):
    inverse_root = lax.rsqrt(jnp.mean(source * source, axis=1, keepdims=True) + EPSILON)
    return (inverse_root, source * inverse_root * gain)


def norm_backward(grad_in, source, inverse_root, gain):
    gain_grad = jnp.sum(grad_in * source * inverse_root, axis=0)
    scaled = grad_in * gain
    inner = jnp.mean(scaled * source, axis=1, keepdims=True)
    return (inverse_root * (scaled - source * inverse_root * inverse_root * inner), gain_grad)


def attend_forward(query, keys, values):
    scores = (
        jnp.einsum("sqkgd,stkd->skgqt", query, keys, preferred_element_type=jnp.float32)
        * SCORE_SCALE
    )
    scores = jnp.where(causal_mask(), scores, NEG_LARGE)
    highest = jnp.max(scores, axis=-1, keepdims=True)
    weights = jnp.exp(scores - highest)
    totals = jnp.sum(weights, axis=-1, keepdims=True)
    log_total = highest + jnp.log(totals)
    probability = (weights / totals).astype(jnp.bfloat16)
    attended = jnp.einsum(
        "skgqt,stkd->sqkgd", probability, values, preferred_element_type=jnp.float32
    )
    return (attended.astype(jnp.bfloat16), log_total)


def attend_backward(query, keys, values, attended, log_total, grad_out):
    scores = (
        jnp.einsum("sqkgd,stkd->skgqt", query, keys, preferred_element_type=jnp.float32)
        * SCORE_SCALE
    )
    scores = jnp.where(causal_mask(), scores, NEG_LARGE)
    probability = jnp.exp(scores - log_total)
    value_grad = jnp.einsum(
        "skgqt,sqkgd->stkd",
        probability.astype(jnp.bfloat16),
        grad_out,
        preferred_element_type=jnp.float32,
    )
    prob_grad = jnp.einsum(
        "sqkgd,stkd->skgqt", grad_out, values, preferred_element_type=jnp.float32
    )
    delta_rows = jnp.sum(grad_out.astype(jnp.float32) * attended.astype(jnp.float32), axis=-1)
    delta_rows = jnp.transpose(delta_rows, (0, 2, 3, 1))[..., None]
    score_grad = (probability * (prob_grad - delta_rows)).astype(jnp.bfloat16)
    query_grad = (
        jnp.einsum("skgqt,stkd->sqkgd", score_grad, keys, preferred_element_type=jnp.float32)
        * SCORE_SCALE
    )
    key_grad = (
        jnp.einsum("skgqt,sqkgd->stkd", score_grad, query, preferred_element_type=jnp.float32)
        * SCORE_SCALE
    )
    return (query_grad, key_grad, value_grad)


MESH = pl.DeviceIdType.MESH


def greet(devices):
    barrier = pltpu.get_barrier_semaphore()
    for device in devices:
        pl.semaphore_signal(barrier, inc=1, device_id=device, device_id_type=MESH)
    pl.semaphore_wait(barrier, len(devices))


def send(source, target, send_sem, recv_sem, device):
    copy = pltpu.make_async_remote_copy(
        src_ref=source,
        dst_ref=target,
        send_sem=send_sem,
        recv_sem=recv_sem,
        device_id=device,
        device_id_type=MESH,
    )
    copy.start()
    return copy


def span(start, size):
    return pl.ds(pl.multiple_of(start, size), size)


def places(n, t):
    me, z = lax.axis_index("dp"), lax.axis_index("tensor")
    core, chip = lax.rem(me, 2), lax.div(me, 2)
    chips = [lax.rem(chip + d, n // 2) for d in range(n // 2)]
    partner = (me + 1 - 2 * core, z)
    peers = [(2 * k + core, z) for k in chips]
    stacked = [(me, lax.rem(z + d, t)) for d in range(t)]
    return me, z, core, chips, partner, peers, stacked


def tensor_stages(t, rows, z, stacked, total, out_ref, slices, s3, r3, s4, r4):
    piece = rows // t
    shared, spread = {}, {}

    def share(c):
        for d in range(1, t):
            shared[c, d] = send(
                total.at[span(c * rows + stacked[d][1] * piece, piece)],
                slices.at[d - 1, span(c * piece, piece)],
                s3.at[c, d - 1],
                r3.at[c, d - 1],
                stacked[d],
            )

    def finish(c):
        mine = span(c * rows + z * piece, piece)
        value = total[mine].astype(jnp.float32)
        for d in range(1, t):
            shared[c, d].wait_recv()
            value = value + slices[d - 1, span(c * piece, piece)].astype(jnp.float32)
        out_ref[mine] = value.astype(out_ref.dtype)
        for d in range(1, t):
            spread[c, d] = send(
                out_ref.at[mine], out_ref.at[mine], s4.at[c, d - 1], r4.at[c, d - 1], stacked[d]
            )

    def drain(c):
        for d in range(1, t):
            spread[c, d].wait_recv()

    def settle():
        for copy in list(shared.values()) + list(spread.values()):
            copy.wait_send()

    return share, finish, drain, settle


def sum_kernel(n, t, chunks, part_ref, out_ref, slices, s3, r3, s4, r4):
    me, z, core, chips, partner, peers, stacked = places(n, t)
    rows = out_ref.shape[0] // chunks
    greet(stacked[1:])
    share, finish, drain, settle = tensor_stages(
        t, rows, z, stacked, part_ref, out_ref, slices, s3, r3, s4, r4
    )
    for c in range(chunks):
        share(c)
    for c in range(chunks):
        finish(c)
    for c in range(chunks):
        drain(c)
    settle()


def reduce_kernel(
    n, t, chunks, part_ref, out_ref, pairs, paired, arrived, total, slices, s1, r1, s2, r2, s3, r3, s4, r4
):
    me, z, core, chips, partner, peers, stacked = places(n, t)
    count = n // 2
    height = out_ref.shape[0]
    rows = height // chunks
    greet([partner] + peers[1:] + stacked[1:])
    share, finish, drain, settle = tensor_stages(
        t, rows, z, stacked, total, out_ref, slices, s3, r3, s4, r4
    )
    order = list(range(1, count)) + [0]
    crossed, passed = {}, {}
    for c in range(chunks):
        for d in order:
            crossed[c, d] = send(
                part_ref.at[span((2 * chips[d] + 1 - core) * height + c * rows, rows)],
                pairs.at[d, pl.ds(c * rows, rows)],
                s1.at[c, d],
                r1.at[c, d],
                partner,
            )

    def pair(c):
        here = pl.ds(c * rows, rows)
        for d in order:
            crossed[c, d].wait_recv()
            kept = part_ref[span((2 * chips[d] + core) * height + c * rows, rows)]
            value = kept.astype(jnp.float32) + pairs[d, here].astype(jnp.float32)
            paired[d, here] = value.astype(paired.dtype)
            if d:
                passed[c, d] = send(
                    paired.at[d, here],
                    arrived.at[d - 1, here],
                    s2.at[c, d - 1],
                    r2.at[c, d - 1],
                    peers[d],
                )

    def collect(c):
        here = pl.ds(c * rows, rows)
        value = paired[0, here].astype(jnp.float32)
        for d in range(1, count):
            passed[c, d].wait_recv()
            value = value + arrived[d - 1, here].astype(jnp.float32)
        total[here] = value.astype(total.dtype)
        share(c)

    for step in range(chunks + 3):
        for late, stage in enumerate((pair, collect, finish, drain)):
            if 0 <= step - late < chunks:
                stage(step - late)
    for copy in list(crossed.values()) + list(passed.values()):
        copy.wait_send()
    settle()


def gather_kernel(n, t, chunks, block_ref, out_ref, s1, r1, s2, r2, s3, r3, local_sem):
    me, z, core, chips, partner, peers, stacked = places(n, t)
    count = n // 2
    height = block_ref.shape[0]
    rows = height // chunks
    greet([partner] + peers[1:])
    direct, forward = {}, {}
    for c in range(chunks):
        for d in range(1, count):
            direct[c, d] = send(
                block_ref.at[pl.ds(c * rows, rows)],
                out_ref.at[span(me * height + c * rows, rows)],
                s1.at[c, d - 1],
                r1.at[c, d - 1],
                peers[d],
            )
    across = send(block_ref, out_ref.at[span(me * height, height)], s3, r3, partner)
    local = pltpu.make_async_copy(block_ref, out_ref.at[span(me * height, height)], local_sem)
    local.start()
    for c in range(chunks):
        for d in range(1, count):
            direct[c, d].wait_recv()
            place = span((2 * chips[count - d] + core) * height + c * rows, rows)
            forward[c, d] = send(
                out_ref.at[place], out_ref.at[place], s2.at[c, d - 1], r2.at[c, d - 1], partner
            )
    for copy in forward.values():
        copy.wait_recv()
    across.wait_recv()
    local.wait()
    for copy in list(direct.values()) + list(forward.values()) + [across]:
        copy.wait_send()


def comm_call(kernel, operand, out_rows, scratch, collective_id):
    n, t = lax.axis_size("dp"), lax.axis_size("tensor")
    chunks = max(SEQ // (16 * t), 1)
    return pl.pallas_call(
        functools.partial(kernel, n, t, chunks),
        out_shape=jax.ShapeDtypeStruct((out_rows, operand.shape[1]), operand.dtype),
        in_specs=[pl.BlockSpec(memory_space=pltpu.VMEM)],
        out_specs=pl.BlockSpec(memory_space=pltpu.VMEM),
        scratch_shapes=scratch(n, t, chunks, operand.shape[1]),
        compiler_params=pltpu.CompilerParams(collective_id=collective_id, has_side_effects=True),
    )(operand)


def twice(*shape):
    return [pltpu.SemaphoreType.DMA(shape), pltpu.SemaphoreType.DMA(shape)]


def sum_scratch(n, t, chunks, width):
    return (
        [pltpu.VMEM((t - 1, SEQ // t, width), jnp.bfloat16)]
        + twice(chunks, t - 1)
        + twice(chunks, t - 1)
    )


def reduce_scratch(n, t, chunks, width):
    half = n // 2
    return (
        [
            pltpu.VMEM((half, SEQ, width), jnp.bfloat16),
            pltpu.VMEM((half, SEQ, width), jnp.bfloat16),
            pltpu.VMEM((half - 1, SEQ, width), jnp.bfloat16),
            pltpu.VMEM((SEQ, width), jnp.bfloat16),
            pltpu.VMEM((t - 1, SEQ // t, width), jnp.bfloat16),
        ]
        + twice(chunks, half)
        + twice(chunks, half - 1)
        + twice(chunks, t - 1)
        + twice(chunks, t - 1)
    )


def gather_scratch(n, t, chunks, width):
    half = n // 2
    return (
        twice(chunks, half - 1)
        + twice(chunks, half - 1)
        + [pltpu.SemaphoreType.DMA] * 3
    )


def gather_rows(block):
    out_rows = block.shape[0] * lax.axis_size("dp")
    return comm_call(gather_kernel, block, out_rows, gather_scratch, 1)


def reduce_rows(partial, collective_id):
    out_rows = partial.shape[0] // lax.axis_size("dp")
    summed = comm_call(reduce_kernel, partial, out_rows, reduce_scratch, collective_id)
    return summed.astype(jnp.float32)


def sum_tensor(partial):
    partial = partial.astype(jnp.bfloat16)
    return comm_call(sum_kernel, partial, partial.shape[0], sum_scratch, 4).astype(jnp.float32)


def spread_columns(per_expert, hidden):
    count = per_expert.shape[1]
    return jnp.concatenate(
        [
            jnp.broadcast_to(per_expert[:, e : e + 1], (per_expert.shape[0], hidden))
            for e in range(count)
        ],
        axis=1,
    )


def layer_forward(inputs, params, local_chosen, cosine, sine):
    (
        attention_gain,
        query_weight,
        key_weight,
        value_weight,
        output_weight,
        mixture_gain,
        router_weight,
        gate_shard,
        up_shard,
        down_shard,
    ) = params
    row_count, width = inputs.shape
    query_heads = query_weight.shape[1] // HD
    key_heads = key_weight.shape[0] // HD
    group_size = query_heads // key_heads
    seq_count = row_count // SEQ
    local_experts, hidden, _ = gate_shard.shape
    first_scale, first_normed = norm_forward(inputs, attention_gain)
    first_input = first_normed.astype(jnp.bfloat16)
    query = jnp.dot(first_input, query_weight, preferred_element_type=jnp.float32).reshape(
        row_count, query_heads, HD
    )
    keys = jnp.dot(first_input, key_weight.T, preferred_element_type=jnp.float32).reshape(
        row_count, key_heads, HD
    )
    values = jnp.dot(first_input, value_weight.T, preferred_element_type=jnp.float32).astype(
        jnp.bfloat16
    )
    query = (query * cosine + rotate_half(query) * sine).astype(jnp.bfloat16)
    keys = (keys * cosine + rotate_half(keys) * sine).astype(jnp.bfloat16)
    query_split = query.reshape(seq_count, SEQ, key_heads, group_size, HD)
    key_split = keys.reshape(seq_count, SEQ, key_heads, HD)
    value_split = values.reshape(seq_count, SEQ, key_heads, HD)
    attended, log_total = attend_forward(query_split, key_split, value_split)
    attended_rows = attended.reshape(row_count, query_heads * HD)
    attention_out = sum_tensor(
        jnp.dot(attended_rows, output_weight, preferred_element_type=jnp.float32)
    )
    middle_state = inputs + RESIDUAL_SCALE * attention_out
    second_scale, second_normed = norm_forward(middle_state, mixture_gain)
    second_input = second_normed.astype(jnp.bfloat16)
    tokens = gather_rows(second_input)
    probs_all = jax.nn.softmax(
        jnp.dot(tokens, router_weight, preferred_element_type=jnp.float32), axis=1
    )
    first_expert = lax.axis_index("dp") * local_experts
    local_weights = local_chosen * lax.dynamic_slice_in_dim(
        probs_all, first_expert, local_experts, axis=1
    )
    weights = spread_columns(local_weights, hidden)
    gate_flat = gate_shard.reshape(local_experts * hidden, width)
    up_flat = up_shard.reshape(local_experts * hidden, width)
    down_flat = down_shard.reshape(local_experts * hidden, width)
    gate_pre = jnp.dot(tokens, gate_flat.T, preferred_element_type=jnp.float32)
    up_pre = jnp.dot(tokens, up_flat.T, preferred_element_type=jnp.float32)
    weighted = (weights * (jax.nn.silu(gate_pre) * up_pre)).astype(jnp.bfloat16)
    partial = jnp.dot(weighted, down_flat, preferred_element_type=jnp.float32).astype(jnp.bfloat16)
    outputs = middle_state + RESIDUAL_SCALE * reduce_rows(partial, 2)
    router_probs = jax.nn.softmax(
        jnp.dot(second_input, router_weight, preferred_element_type=jnp.float32), axis=1
    )
    saved = (
        first_scale,
        first_input,
        query_split,
        key_split,
        value_split,
        attended,
        log_total,
        middle_state,
        second_scale,
        second_input,
        router_probs,
        weights,
        tokens,
        gate_pre,
        up_pre,
        weighted,
    )
    return (outputs, saved)


def layer_backward(grad_out, grads, saved, params, chosen, cosine, sine, inputs):
    (
        attention_gain,
        query_weight,
        key_weight,
        value_weight,
        output_weight,
        mixture_gain,
        router_weight,
        gate_shard,
        up_shard,
        down_shard,
    ) = params
    (
        first_scale,
        first_input,
        query_split,
        key_split,
        value_split,
        attended,
        log_total,
        middle_state,
        second_scale,
        second_input,
        router_probs,
        weights,
        tokens,
        gate_pre,
        up_pre,
        weighted,
    ) = saved
    row_count, width = grad_out.shape
    query_heads = query_weight.shape[1] // HD
    key_heads = key_weight.shape[0] // HD
    local_experts, hidden, _ = gate_shard.shape
    expert_count = router_weight.shape[1]
    gate_flat = gate_shard.reshape(local_experts * hidden, width)
    up_flat = up_shard.reshape(local_experts * hidden, width)
    down_flat = down_shard.reshape(local_experts * hidden, width)
    if grads is None:
        grads = gather_rows((RESIDUAL_SCALE * grad_out).astype(jnp.bfloat16))
    back = jnp.dot(grads, down_flat.T, preferred_element_type=jnp.float32)
    sigma = jax.nn.sigmoid(gate_pre)
    products = gate_pre * sigma * up_pre * back
    weight_part = jnp.concatenate(
        [
            jnp.sum(products[:, e * hidden : (e + 1) * hidden], axis=1, keepdims=True)
            for e in range(local_experts)
        ],
        axis=1,
    )
    act_grad = weights * back
    gate_rows = (act_grad * up_pre * sigma * (1.0 + gate_pre * (1.0 - sigma))).astype(jnp.bfloat16)
    up_rows = (act_grad * gate_pre * sigma).astype(jnp.bfloat16)
    dispatch_part = jnp.dot(gate_rows, gate_flat, preferred_element_type=jnp.float32) + jnp.dot(
        up_rows, up_flat, preferred_element_type=jnp.float32
    )
    first_expert = lax.axis_index("dp") * local_experts
    side = lax.dynamic_update_slice_in_dim(
        jnp.zeros((tokens.shape[0], 128), jnp.float32), weight_part, first_expert, axis=1
    )
    summed = reduce_rows(
        jnp.concatenate([dispatch_part, side], axis=1).astype(jnp.bfloat16), 3
    )
    down_grad = jnp.dot(weighted.T, grads, preferred_element_type=jnp.float32)
    gate_grad = jnp.dot(gate_rows.T, tokens, preferred_element_type=jnp.float32)
    up_grad = jnp.dot(up_rows.T, tokens, preferred_element_type=jnp.float32)
    router_float = router_weight.astype(jnp.float32)
    prob_grad = chosen * summed[:, width : width + expert_count]
    logit_grad = router_probs * (
        prob_grad - jnp.sum(router_probs * prob_grad, axis=1, keepdims=True)
    )
    second_grad = summed[:, :width] + dot_full(logit_grad, router_float.T)
    router_grad = dot_full(second_input.astype(jnp.float32).T, logit_grad)
    middle_norm_grad, mixture_gain_grad = norm_backward(
        second_grad, middle_state, second_scale, mixture_gain
    )
    middle_grad = grad_out + middle_norm_grad
    attention_grad = (RESIDUAL_SCALE * middle_grad).astype(jnp.bfloat16)
    attended_rows = attended.reshape(row_count, query_heads * HD)
    output_grad = jnp.dot(attention_grad.T, attended_rows, preferred_element_type=jnp.float32)
    attended_grad = jnp.dot(
        attention_grad, output_weight.T, preferred_element_type=jnp.float32
    ).astype(jnp.bfloat16)
    query_grad, key_grad, value_grad = attend_backward(
        query_split,
        key_split,
        value_split,
        attended,
        log_total,
        attended_grad.reshape(attended.shape),
    )
    query_grad = query_grad.reshape(row_count, query_heads, HD)
    query_grad = (
        (query_grad * cosine - rotate_half(query_grad) * sine)
        .astype(jnp.bfloat16)
        .reshape(row_count, query_heads * HD)
    )
    key_grad = key_grad.reshape(row_count, key_heads, HD)
    key_grad = (
        (key_grad * cosine - rotate_half(key_grad) * sine)
        .astype(jnp.bfloat16)
        .reshape(row_count, key_heads * HD)
    )
    value_grad = value_grad.astype(jnp.bfloat16).reshape(row_count, key_heads * HD)
    first_part = (
        jnp.dot(query_grad, query_weight.T, preferred_element_type=jnp.float32)
        + jnp.dot(key_grad, key_weight, preferred_element_type=jnp.float32)
        + jnp.dot(value_grad, value_weight, preferred_element_type=jnp.float32)
    )
    first_grad = sum_tensor(first_part)
    input_norm_grad, attention_gain_grad = norm_backward(
        first_grad, inputs, first_scale, attention_gain
    )
    input_grad = middle_grad + input_norm_grad
    projected = jnp.dot(
        first_input.T,
        jnp.concatenate([query_grad, key_grad, value_grad], axis=1),
        preferred_element_type=jnp.float32,
    )
    small = jnp.concatenate(
        [
            router_grad,
            attention_gain_grad[:, None],
            mixture_gain_grad[:, None],
            jnp.zeros((width, 126 - expert_count), jnp.float32),
        ],
        axis=1,
    )
    dense = lax.psum_scatter(
        jnp.concatenate([projected, output_grad, small], axis=1).astype(jnp.bfloat16),
        "dp",
        scatter_dimension=0,
        tiled=True,
    ).astype(jnp.float32)
    q, k = query_heads * HD, key_heads * HD
    side = dense[:, 2 * q + 2 * k :]
    dense = (
        side[:, expert_count],
        dense[:, :q],
        dense[:, q : q + k].T,
        dense[:, q + k : q + 2 * k].T,
        dense[:, q + 2 * k : 2 * q + 2 * k].T,
        side[:, expert_count + 1],
        side[:, :expert_count],
    )
    experts = tuple(entry.reshape(gate_shard.shape) for entry in (gate_grad, up_grad, down_grad))
    return (input_grad, dense, experts)


def shards(
    hidden_states,
    output_cotangent,
    routes,
    attention_gain,
    query_weight,
    key_weight,
    value_weight,
    output_weight,
    mixture_gain,
    router_weight,
    gate_weight,
    up_weight,
    down_weight,
):
    params_all = (
        attention_gain,
        query_weight,
        key_weight,
        value_weight,
        output_weight,
        mixture_gain,
        router_weight,
        gate_weight,
        up_weight,
        down_weight,
    )
    row_count = hidden_states.shape[0]
    layer_count = query_weight.shape[0]
    cosine, sine = rope_tables(row_count)
    local_experts = gate_weight.shape[1]
    expert_ids = jnp.arange(EXPERTS, dtype=jnp.int32)
    chosen = jnp.any(routes[:, :, None] == expert_ids[None, None, :], axis=1).astype(jnp.float32)
    local_ids = lax.axis_index("dp") * local_experts + jnp.arange(local_experts, dtype=jnp.int32)
    routes_all = lax.all_gather(routes, "dp", axis=0, tiled=True)
    local_chosen = jnp.any(routes_all[:, :, None] == local_ids[None, None, :], axis=1).astype(
        jnp.float32
    )
    current = hidden_states
    kept = []
    for layer_index in range(layer_count):
        layer_params = tuple((weight[layer_index] for weight in params_all))
        layer_input = current
        current, saved = layer_forward(current, layer_params, local_chosen, cosine, sine)
        kept.append((saved, layer_input))
    grad_now = output_cotangent
    gathered = lax.all_gather(
        (RESIDUAL_SCALE * output_cotangent).astype(jnp.bfloat16), "dp", axis=0, tiled=True
    )
    dense_layers = [None] * layer_count
    expert_layers = [None] * layer_count
    for layer_index in reversed(range(layer_count)):
        layer_params = tuple((weight[layer_index] for weight in params_all))
        grad_now, dense, expert_grads = layer_backward(
            grad_now,
            gathered,
            kept[layer_index][0],
            layer_params,
            chosen,
            cosine,
            sine,
            kept[layer_index][1],
        )
        gathered = None
        dense_layers[layer_index] = dense
        expert_layers[layer_index] = expert_grads
    stacked = tuple(
        (jnp.stack([entry[position] for entry in dense_layers]) for position in range(7))
    )
    experts_stacked = tuple(
        (jnp.stack([entry[position] for entry in expert_layers]) for position in range(3))
    )
    return (
        current,
        grad_now,
        stacked[0],
        stacked[1],
        stacked[2],
        stacked[3],
        stacked[4],
        stacked[5],
        stacked[6],
        experts_stacked[0],
        experts_stacked[1],
        experts_stacked[2],
    )


def solution(mesh):
    placed = (
        P("dp", None),
        P("dp", None),
        P("dp", None),
        P(),
        P(None, None, "tensor"),
        P(None, "tensor", None),
        P(None, "tensor", None),
        P(None, "tensor", None),
        P(),
        P(),
        P(None, "dp", "tensor", None),
        P(None, "dp", "tensor", None),
        P(None, "dp", "tensor", None),
    )
    return jax.shard_map(
        shards,
        mesh=mesh,
        in_specs=placed,
        out_specs=(
            P("dp", None),
            P("dp", None),
            P(None, "dp"),
            P(None, "dp", "tensor"),
            P(None, "tensor", "dp"),
            P(None, "tensor", "dp"),
            P(None, "tensor", "dp"),
            P(None, "dp"),
            P(None, "dp", None),
            P(None, "dp", "tensor", None),
            P(None, "dp", "tensor", None),
            P(None, "dp", "tensor", None),
        ),
        check_vma=False,
    )
```
